1024 devices in a mesh: phase: 8 (over x), blk: 32 (over z_hi, y), head: 4 (over z_lo, core).
Axes of the slice: x: 8, y: 8, z: 8 (z_hi: 4, z_lo: 2; z = z_hi * 2 + z_lo), core: 2. Of those that a mesh axis runs over, the one named last changes fastest.
Arguments:
- visual: bfloat16 [131072, 4096], P(('phase', 'blk')), may hold values from -8 to 8
- key_weight: bfloat16 [4096, 1024], P(None, 'head'), may hold values from -1 to 1
- value_weight: bfloat16 [4096, 1024], P(None, 'head'), may hold values from -0.09375 to 0.09375
- queries: bfloat16 [512, 4096], P('blk', 'head'), may hold values from -512 to 512
- bounds: int32 [512, 2], P('blk'), may hold values from 0 to 131072, as said below
- tile_mask: int32 [32, 256], replicated, may hold values from 0 to 1
Outputs:
- attended: bfloat16 [512, 4096], P('blk', 'head')
The draws below stay inside these ranges and needn't reach their ends.
Inputs may be any that keep to these rules, and one draw needn't show every extreme that they name: For each text row 0 <= bounds[i, 0] < bounds[i, 1] <= 131072; the first row starts at 0 and the last ends at 131072; every text row may see all 512 rows of at least one visual tile.
All inputs are finite; a program needn't handle non-finite values.
Results may differ from the reference program's by a relative error of at most 0.015.
Values may be sent and summed in bfloat16 or wider, within the bound.
No kernel may reach another device: no remote copies, remote signals or barrier semaphores. Data moves between devices by JAX's collectives and lax.ppermute only.
A program may use at most 32 MiB of HBM per device.

```python
import math
import jax
import jax.numpy as jnp
from jax import lax

D = 4096
HD = 128
QH = 32
KVH = 8
VIS_DEV = 512
TXT_DEV = 16
TEXT = 512
NV = 131072
TTILES = 32
VTILES = 256
QW = 4096
KVW = 1024


def plan_helper(key):
    base = jax.random.fold_in(key, 7001)
    first_key, second_key, third_key, fourth_key = jax.random.split(base, 4)
    anchor = jax.random.randint(first_key, (TTILES,), 0, VTILES)
    coin = jax.random.randint(second_key, (TTILES, VTILES), 0, 5)
    tiles = jnp.arange(VTILES)[None, :]
    mask = jnp.where((coin < 2) | (tiles == anchor[:, None]), 1, 0).astype(jnp.int32)
    rows = jnp.arange(TEXT)
    start = anchor[rows // TXT_DEV] * VIS_DEV
    reach = NV // 2 + 1
    lower = jnp.maximum(start - jax.random.randint(third_key, (TEXT,), 0, reach), 0)
    upper = jnp.minimum(start + VIS_DEV + jax.random.randint(fourth_key, (TEXT,), 0, reach), NV)
    lower = jnp.where(rows == 0, 0, lower)
    upper = jnp.where(rows == TEXT - 1, NV, upper)
    return (mask, jnp.stack([lower, upper], axis=1).astype(jnp.int32))


def visual_row(key, row_number):
    row_key = jax.random.fold_in(jax.random.fold_in(key, 7002), row_number)
    return jnp.clip(jax.random.normal(row_key, (D,), jnp.float32), -6.0, 6.0)


def key_matrix(key):
    raw = jax.random.normal(jax.random.fold_in(key, 7003), (D, KVW), jnp.float32)
    return (jnp.clip(raw, -6.0, 6.0) / math.sqrt(D)).astype(jnp.bfloat16)


def draw_visual(key, part):

    def inner(row_number):
        return visual_row(key, row_number)
    return jax.vmap(inner)(jnp.arange(NV)).astype(jnp.bfloat16)


def draw_key_weight(key, part):
    return key_matrix(key)


def draw_bounds(key, part):
    return plan_helper(key)[1]


def draw_tile_mask(key, part):
    return plan_helper(key)[0]


def draw_queries(key, part):
    drawn = jnp.clip(jax.random.normal(jax.random.fold_in(key, 7004), (TEXT, QW), jnp.float32), -6.0, 6.0)
    return drawn.astype(jnp.bfloat16)


def block_levels(own_key, dims, cuts, low, high):
    def one(dim, blocks):
        draws = jax.random.uniform(jax.random.fold_in(jax.random.fold_in(own_key, 6), dim), (blocks,), jnp.float32, low / len(cuts), high / len(cuts))
        return jnp.repeat(jnp.exp(draws), dims[dim] // blocks).reshape((-1,) + (1,) * (len(dims) - dim - 1))

    level = one(*cuts[0])
    for cut in cuts[1:]:
        level = level * one(*cut)
    return level


def centred(stream_key, shape, scale, most, pieces=(), held_as=jnp.bfloat16):
    loudness = block_levels(stream_key, shape, pieces, -0.22, 0.18) if pieces else 1.0
    values = jax.random.normal(stream_key, shape, jnp.float32) * scale * loudness
    return jnp.minimum(jnp.maximum(values, -most), most).astype(held_as)


def setup_inputs(seed: int = 0) -> dict:
    seeds = jax.random.split(jax.random.key(seed), 7)
    return {
        "visual": draw_visual(jax.random.fold_in(seeds[6], 71), 0),
        "key_weight": draw_key_weight(jax.random.fold_in(seeds[6], 71), 0),
        "value_weight": centred(seeds[2], (D, KVW), D ** -0.5, 0.09375, ((1, 4),)),
        "queries": draw_queries(jax.random.fold_in(seeds[6], 71), 0),
        "bounds": draw_bounds(jax.random.fold_in(seeds[6], 71), 0),
        "tile_mask": draw_tile_mask(jax.random.fold_in(seeds[6], 71), 0),
    }


def reference(visual, key_weight, value_weight, queries, bounds, tile_mask):
    keys = jnp.dot(visual, key_weight, preferred_element_type=jnp.float32).astype(jnp.bfloat16)
    values = jnp.dot(visual, value_weight, preferred_element_type=jnp.float32).astype(jnp.bfloat16)
    text_index = jnp.arange(TEXT, dtype=jnp.int32)
    vis_index = jnp.arange(NV, dtype=jnp.int32)
    lower = bounds[:, 0]
    upper = bounds[:, 1]
    tile_rows = tile_mask[text_index // TXT_DEV]
    tile_bits = tile_rows[:, vis_index // VIS_DEV]
    permitted = (vis_index[None, :] >= lower[:, None]) & (vis_index[None, :] < upper[:, None]) & (tile_bits == 1)
    group = QH // KVH
    scale = 1.0 / math.sqrt(HD)

    def one_head(head_number):
        kv_number = head_number // group
        query_head = lax.dynamic_slice_in_dim(queries, (head_number * HD).astype(jnp.int32), HD, 1)
        key_head = lax.dynamic_slice_in_dim(keys, (kv_number * HD).astype(jnp.int32), HD, 1)
        value_head = lax.dynamic_slice_in_dim(values, (kv_number * HD).astype(jnp.int32), HD, 1)
        scores = jnp.dot(query_head, key_head.T, preferred_element_type=jnp.float32) * scale
        masked = jnp.where(permitted, scores, -1e+30)
        row_top = lax.optimization_barrier(jnp.max(masked, axis=1))
        weights = jnp.where(permitted, jnp.exp(masked - row_top[:, None]), 0.0)
        row_total = lax.optimization_barrier(jnp.sum(weights, axis=1))
        summed = jnp.dot(weights.astype(jnp.bfloat16), value_head, preferred_element_type=jnp.float32)
        return summed / row_total[:, None]
    heads_out = lax.map(one_head, jnp.arange(QH, dtype=jnp.int32))
    attended = jnp.transpose(heads_out, (1, 0, 2)).reshape(TEXT, QH * HD)
    return attended.astype(jnp.bfloat16)
```

```python
import math

import jax
import jax.numpy as jnp
from jax import lax
from jax.experimental import pallas as pl
from jax.experimental.pallas import tpu as pltpu
from jax.sharding import PartitionSpec as P

HD = 128
LANES = 128
HIDDEN = -1e30
FLOOR = -1e29
RATE = math.log2(math.e) / math.sqrt(HD)
F32 = jnp.float32
BF16 = jnp.bfloat16
VMEM = pl.BlockSpec(memory_space=pltpu.VMEM)
SMEM = pl.BlockSpec(memory_space=pltpu.SMEM)


def lane_ids(rows):
    return lax.broadcasted_iota(jnp.int32, (rows, LANES), 1)


def row_ids(rows):
    return lax.broadcasted_iota(jnp.int32, (rows, LANES), 0)


def split3(x):
    first = x.astype(BF16).astype(F32)
    rest = x - first
    second = rest.astype(BF16).astype(F32)
    return first, second, (rest - second).astype(BF16).astype(F32)


def stats_block(top, total):
    parts = split3(top) + split3(total)
    rows = row_ids(16)
    block = jnp.zeros((16, LANES), F32)
    for number, part in enumerate(parts):
        block = jnp.where(rows == number, part, block)
    return block.astype(BF16)


def read_stats(block):
    block = block.astype(F32)
    top = block[0:1] + block[1:2] + block[2:3]
    total = block[3:4] + block[4:5] + block[5:6]
    return top, total


def pack_kernel(q_ref, bounds_ref, out_ref):
    heads = q_ref.shape[1] // HD
    rows = q_ref.shape[0]
    blocks = [q_ref[:, h * HD:(h + 1) * HD] for h in range(heads)]
    bounds = bounds_ref[...]
    lanes = lane_ids(rows)
    tail = jnp.zeros((rows, LANES), F32)
    for side in range(2):
        value = bounds[:, side:side + 1]
        pieces = (value >> 9, (value >> 1) & 255, value & 1)
        for number, piece in enumerate(pieces):
            tail = jnp.where(lanes == 3 * side + number, piece.astype(F32), tail)
    blocks.append(tail.astype(BF16))
    packed = jnp.concatenate(blocks, axis=0)
    for copy in range(out_ref.shape[0]):
        out_ref[copy] = packed


def project_kernel(x_ref, kw_ref, vw_ref, k_ref, v_ref, k_acc, v_acc):
    step = pl.program_id(0)

    @pl.when(step == 0)
    def _():
        k_acc[...] = jnp.zeros_like(k_acc)
        v_acc[...] = jnp.zeros_like(v_acc)

    x = x_ref[...]
    k_acc[...] += jnp.dot(x, kw_ref[...], preferred_element_type=F32)
    v_acc[...] += jnp.dot(x, vw_ref[...], preferred_element_type=F32)

    @pl.when(step == pl.num_programs(0) - 1)
    def _():
        k_ref[...] = k_acc[...].astype(BF16)
        v_ref[...] = v_acc[...].astype(BF16)


def attend_kernel(bits_ref, start_ref, q_ref, k_ref, v_ref, out_ref):
    tiles = q_ref.shape[0]
    vis = k_ref.shape[0]
    kv_heads = k_ref.shape[1] // HD
    text = 16
    group_rows = LANES // kv_heads
    columns = (lax.broadcasted_iota(jnp.int32, (text, vis), 1) + start_ref[0]).astype(F32)

    def tile_step(t, _):
        @pl.when(bits_ref[t] == 1)
        def _():
            edges = q_ref[t, LANES:, :].astype(F32)
            lower = edges[:, 0:1] * 512 + edges[:, 1:2] * 2 + edges[:, 2:3]
            upper = edges[:, 3:4] * 512 + edges[:, 4:5] * 2 + edges[:, 5:6]
            visible = (columns >= lower) & (columns < upper)
            bias = jnp.where(visible, 0.0, HIDDEN)
            tops, totals = [], []
            for kv in range(kv_heads):
                rows = slice(kv * group_rows, (kv + 1) * group_rows)
                heads = slice(kv * HD, (kv + 1) * HD)
                scores = lax.dot_general(
                    q_ref[t, rows, :], k_ref[:, heads], (((1,), (1,)), ((), ())),
                    preferred_element_type=F32,
                )
                scores = (scores.reshape(group_rows // text, text, vis) + bias[None]).reshape(
                    group_rows, vis
                )
                top = jnp.maximum(jnp.max(scores, axis=1, keepdims=True), FLOOR)
                weights = jnp.exp2((scores - top) * RATE)
                totals.append(jnp.sum(weights, axis=1, keepdims=True))
                tops.append(top)
                summed = jnp.dot(
                    weights.astype(BF16), v_ref[:, heads], preferred_element_type=F32
                )
                out_ref[t, rows, :] = summed.astype(BF16)
            lanes = lane_ids(LANES)
            top = jnp.concatenate(tops, axis=0)
            total = jnp.concatenate(totals, axis=0)
            both = jnp.where(lanes == 0, top, jnp.where(lanes == 1, total, 0.0)).T
            out_ref[t, LANES:, :] = stats_block(both[0:1], both[1:2])

        @pl.when(bits_ref[t] != 1)
        def _():
            out_ref[t, :LANES, :] = jnp.zeros((LANES, LANES), BF16)
            out_ref[t, LANES:, :] = stats_block(
                jnp.full((1, LANES), FLOOR, F32), jnp.zeros((1, LANES), F32)
            )

        return 0

    lax.fori_loop(0, tiles, tile_step, 0)


def joined(ref):
    n = ref.shape[0]
    stats = [read_stats(ref[s, LANES:, :]) for s in range(n)]
    tops = jnp.concatenate([top for top, _ in stats], axis=0)
    totals = jnp.concatenate([total for _, total in stats], axis=0)
    top = jnp.max(tops, axis=0, keepdims=True)
    factors = jnp.exp2((tops - top) * RATE)
    total = jnp.sum(factors * totals, axis=0, keepdims=True)
    padded = jnp.concatenate([factors, total, jnp.zeros((LANES - n - 1, LANES), F32)], axis=0).T
    summed = jnp.zeros((LANES, LANES), F32)
    for s in range(n):
        summed += padded[:, s:s + 1] * ref[s, :LANES, :].astype(F32)
    return top, total, padded[:, n:n + 1], summed


def join_kernel(in_ref, out_ref):
    top, total, _, summed = joined(in_ref)
    piece = jnp.concatenate([summed.astype(BF16), stats_block(top, total)], axis=0)
    for copy in range(out_ref.shape[0]):
        out_ref[copy] = piece


def finish_kernel(in_ref, out_ref):
    _, _, total, summed = joined(in_ref)
    result = (summed / total).astype(BF16)
    rows = out_ref.shape[0]
    for h in range(out_ref.shape[1] // HD):
        out_ref[:, h * HD:(h + 1) * HD] = result[h * rows:(h + 1) * rows]


def per_device(visual, key_weight, value_weight, queries, bounds, tile_mask):
    vis_rows, depth = visual.shape
    width = key_weight.shape[1]
    text_rows = queries.shape[0]
    blocks = lax.axis_size("blk")
    phases = lax.axis_size("phase")
    my_tile = lax.axis_index("phase") * blocks + lax.axis_index("blk")
    piece_rows = LANES + 16

    def exchange(pieces, axis):
        return lax.all_to_all(pieces, axis, 0, 0, tiled=True)

    packed = pl.pallas_call(
        pack_kernel,
        out_shape=jax.ShapeDtypeStruct((blocks, piece_rows, LANES), BF16),
        in_specs=[VMEM, VMEM],
        out_specs=VMEM,
    )(queries, bounds)
    gathered = exchange(packed, "blk")

    chunk = 512
    keys, values = pl.pallas_call(
        project_kernel,
        grid=(depth // chunk,),
        in_specs=[
            pl.BlockSpec((vis_rows, chunk), lambda i: (0, i)),
            pl.BlockSpec((chunk, width), lambda i: (i, 0)),
            pl.BlockSpec((chunk, width), lambda i: (i, 0)),
        ],
        out_specs=[pl.BlockSpec((vis_rows, width), lambda i: (0, 0))] * 2,
        out_shape=[jax.ShapeDtypeStruct((vis_rows, width), BF16)] * 2,
        scratch_shapes=[pltpu.VMEM((vis_rows, width), F32)] * 2,
        compiler_params=pltpu.CompilerParams(dimension_semantics=("arbitrary",)),
        cost_estimate=pl.CostEstimate(
            flops=4 * vis_rows * depth * width,
            bytes_accessed=2 * depth * (vis_rows + 2 * width),
            transcendentals=0,
        ),
    )(visual, key_weight, value_weight)

    tile_ids = lax.broadcasted_iota(jnp.int32, tile_mask.shape, 1)
    bits = jnp.sum(jnp.where(tile_ids == my_tile, tile_mask, 0), axis=1)
    start = (my_tile * vis_rows).astype(jnp.int32).reshape(1)
    partials = pl.pallas_call(
        attend_kernel,
        out_shape=jax.ShapeDtypeStruct((blocks, piece_rows, LANES), BF16),
        in_specs=[SMEM, SMEM, VMEM, VMEM, VMEM],
        out_specs=VMEM,
    )(bits, start, gathered, keys, values)

    partials = exchange(partials, "blk")
    section = pl.pallas_call(
        join_kernel,
        out_shape=jax.ShapeDtypeStruct((phases, piece_rows, LANES), BF16),
        in_specs=[VMEM],
        out_specs=VMEM,
    )(partials)
    sections = exchange(section, "phase")
    return pl.pallas_call(
        finish_kernel,
        out_shape=jax.ShapeDtypeStruct(queries.shape, BF16),
        in_specs=[VMEM],
        out_specs=VMEM,
    )(sections)


def solution(mesh):
    return jax.shard_map(
        per_device,
        mesh=mesh,
        in_specs=(
            P(("phase", "blk"), None),
            P(None, "head"),
            P(None, "head"),
            P("blk", "head"),
            P("blk", None),
            P(),
        ),
        out_specs=P("blk", "head"),
        check_vma=False,
    )
```

```python
import math

import jax
import jax.numpy as jnp
from jax import lax
from jax.experimental import pallas as pl
from jax.experimental.pallas import tpu as pltpu
from jax.sharding import PartitionSpec as P

HD = 128
LANES = 128
HIDDEN = -1e30
FLOOR = -1e29
RATE = math.log2(math.e) / math.sqrt(HD)
F32 = jnp.float32
BF16 = jnp.bfloat16
VMEM = pl.BlockSpec(memory_space=pltpu.VMEM)
SMEM = pl.BlockSpec(memory_space=pltpu.SMEM)


def lane_ids(rows):
    return lax.broadcasted_iota(jnp.int32, (rows, LANES), 1)


def row_ids(rows):
    return lax.broadcasted_iota(jnp.int32, (rows, LANES), 0)


def split3(x):
    first = x.astype(BF16).astype(F32)
    rest = x - first
    second = rest.astype(BF16).astype(F32)
    return first, second, (rest - second).astype(BF16).astype(F32)


def stats_block(top, total):
    parts = split3(top) + split3(total)
    rows = row_ids(16)
    block = jnp.zeros((16, LANES), F32)
    for number, part in enumerate(parts):
        block = jnp.where(rows == number, part, block)
    return block.astype(BF16)


def read_stats(block):
    block = block.astype(F32)
    top = block[0:1] + block[1:2] + block[2:3]
    total = block[3:4] + block[4:5] + block[5:6]
    return top, total


def pack_kernel(side_ref, q_ref, bounds_ref, out_ref):
    rows = q_ref.shape[0]
    width = q_ref.shape[1] // 2
    first = side_ref[0] * width
    blocks = [
        q_ref[:, pl.ds(pl.multiple_of(first + g * HD, HD), HD)] for g in range(width // HD)
    ]
    bounds = bounds_ref[...]
    lanes = lane_ids(rows)
    tail = jnp.zeros((rows, LANES), F32)
    for side in range(2):
        value = bounds[:, side:side + 1]
        pieces = (value >> 9, (value >> 1) & 255, value & 1)
        for number, piece in enumerate(pieces):
            tail = jnp.where(lanes == 3 * side + number, piece.astype(F32), tail)
    blocks.append(tail.astype(BF16))
    packed = jnp.concatenate(blocks, axis=0)
    for copy in range(out_ref.shape[0]):
        out_ref[copy] = packed


def project_kernel(side_ref, x_ref, kw_ref, vw_ref, keep_ref, send_ref, k_acc, v_acc):
    step = pl.program_id(0)

    @pl.when(step == 0)
    def _():
        k_acc[...] = jnp.zeros_like(k_acc)
        v_acc[...] = jnp.zeros_like(v_acc)

    x = x_ref[...]
    k_acc[...] += jnp.dot(x, kw_ref[...], preferred_element_type=F32)
    v_acc[...] += jnp.dot(x, vw_ref[...], preferred_element_type=F32)

    for side in range(2):
        @pl.when((step == pl.num_programs(0) - 1) & (side_ref[0] == side))
        def _():
            for head, out_ref in ((side, keep_ref), (1 - side, send_ref)):
                columns = slice(head * HD, (head + 1) * HD)
                out_ref[0] = k_acc[:, columns].astype(BF16)
                out_ref[1] = v_acc[:, columns].astype(BF16)


def attend_kernel(tiles_ref, bits_ref, q_ref, own_ref, other_ref, out_ref):
    pairs, _, piece, _ = q_ref.shape
    text = 16
    rows = piece - text
    group = rows // text
    vis = own_ref.shape[1]
    columns = lax.broadcasted_iota(jnp.int32, (text, vis), 1).astype(F32)

    def pair_step(pair, _):
        edges = []
        for half in range(2):
            digits = q_ref[pair, half, rows:, :].astype(F32)
            lower = digits[:, 0:1] * 512 + digits[:, 1:2] * 2 + digits[:, 2:3]
            upper = digits[:, 3:4] * 512 + digits[:, 4:5] * 2 + digits[:, 5:6]
            edges.append((lower, upper))
        queries = jnp.concatenate([q_ref[pair, half, :rows, :] for half in range(2)], axis=0)
        scores, tops = [], []
        for source, kv_ref in enumerate((own_ref, other_ref)):
            start = (tiles_ref[source] * vis).astype(F32)
            found = lax.dot_general(
                queries, kv_ref[0], (((1,), (1,)), ((), ())), preferred_element_type=F32
            ).reshape(2, group, text, vis)
            parts = []
            for half in range(2):
                lower, upper = edges[half]
                bit = bits_ref[source, 2 * pair + half]
                hidden = (1 - bit).astype(F32) * 1e7
                visible = (columns >= lower - start + hidden) & (columns < upper - start)
                bias = jnp.where(visible, 0.0, HIDDEN)
                parts.append(found[half] + bias[None])
            masked = jnp.stack(parts).reshape(2 * rows, vis)
            scores.append(masked)
            tops.append(jnp.max(masked, axis=1, keepdims=True))
        top = jnp.maximum(jnp.maximum(tops[0], tops[1]), FLOOR)
        total = jnp.zeros((2 * rows, 1), F32)
        summed = jnp.zeros((2 * rows, HD), F32)
        for masked, kv_ref in zip(scores, (own_ref, other_ref)):
            weights = jnp.exp2((masked - top) * RATE)
            total += jnp.sum(weights, axis=1, keepdims=True)
            summed += jnp.dot(weights.astype(BF16), kv_ref[1], preferred_element_type=F32)
        out_ref[pair, :LANES, :] = summed.astype(BF16)
        lanes = lane_ids(LANES)
        both = jnp.where(lanes == 0, top, jnp.where(lanes == 1, total, 0.0)).T
        out_ref[pair, LANES:, :] = stats_block(both[0:1], both[1:2])
        return 0

    lax.fori_loop(0, pairs, pair_step, 0, unroll=2)


def joined(pieces):
    n = len(pieces)
    rows = pieces[0].shape[0] - 16
    stats = [read_stats(piece[rows:, :]) for piece in pieces]
    tops = jnp.concatenate([top for top, _ in stats], axis=0)
    totals = jnp.concatenate([total for _, total in stats], axis=0)
    top = jnp.max(tops, axis=0, keepdims=True)
    factors = jnp.exp2((tops - top) * RATE)
    total = jnp.sum(factors * totals, axis=0, keepdims=True)
    spread = jnp.concatenate([factors, total, jnp.zeros((LANES - n - 1, LANES), F32)], axis=0).T
    summed = jnp.zeros((rows, LANES), F32)
    for s in range(n):
        summed += spread[:rows, s:s + 1] * pieces[s][:rows, :].astype(F32)
    return top, total, spread[:rows, n:n + 1], summed


def join_pairs_kernel(in_ref, out_ref):
    sources, pairs = in_ref.shape[:2]
    rows = out_ref.shape[1] - 16
    for pair in range(pairs):
        top, total, _, summed = joined([in_ref.at[s, pair] for s in range(sources)])
        summed = summed.astype(BF16)
        for half in range(2):
            cut = slice(half * rows, (half + 1) * rows)
            out_ref[2 * pair + half, :rows, :] = summed[cut]
            if half == 0:
                stats = stats_block(top, total)
            else:
                stats = stats_block(pltpu.roll(top, rows, 1), pltpu.roll(total, rows, 1))
            out_ref[2 * pair + half, rows:, :] = stats


def join_kernel(in_ref, out_ref):
    top, total, _, summed = joined([in_ref.at[s] for s in range(in_ref.shape[0])])
    piece = jnp.concatenate([summed.astype(BF16), stats_block(top, total)], axis=0)
    for copy in range(out_ref.shape[0]):
        out_ref[copy] = piece


def finish_kernel(in_ref, out_ref):
    sources = in_ref.shape[0]
    text = out_ref.shape[0]
    for side in range(2):
        _, _, total, summed = joined([in_ref.at[s] for s in range(side, sources, 2)])
        result = (summed / total).astype(BF16)
        group = result.shape[0] // text
        for g in range(group):
            first = (side * group + g) * HD
            out_ref[:, first:first + HD] = result[g * text:(g + 1) * text]


def call(kernel, out, in_specs):
    return pl.pallas_call(
        kernel, out_shape=jax.ShapeDtypeStruct(out, BF16), in_specs=in_specs, out_specs=VMEM
    )


def per_device(visual, key_weight, value_weight, queries, bounds, tile_mask):
    vis_rows, depth = visual.shape
    width = key_weight.shape[1]
    text = queries.shape[0]
    rows = queries.shape[1] // HD // 2 * text
    piece = rows + text
    zs, ys = lax.axis_size("zh"), lax.axis_size("y")
    phases = lax.axis_size("xh") * 2
    side = lax.axis_index("xl")
    blk = lax.axis_index("zh") * ys + lax.axis_index("y")
    phase = lax.axis_index("xh") * 2 + side
    tiles = jnp.stack([phase * (zs * ys) + blk, (phase ^ 1) * (zs * ys) + blk])
    side = side.reshape(1)

    def exchange(pieces, axis):
        return lax.all_to_all(pieces, axis, 0, 0, tiled=True)

    packed = call(pack_kernel, (zs, piece, LANES), [SMEM, VMEM, VMEM])(side, queries, bounds)
    column = exchange(packed, "zh")
    gathered = exchange(jnp.broadcast_to(column[None], (ys,) + column.shape), "y")

    chunk = 512
    half = pl.BlockSpec((2, vis_rows, HD), lambda i: (0, 0, 0))
    keep, send = pl.pallas_call(
        project_kernel,
        grid=(depth // chunk,),
        in_specs=[
            SMEM,
            pl.BlockSpec((vis_rows, chunk), lambda i: (0, i)),
            pl.BlockSpec((chunk, width), lambda i: (i, 0)),
            pl.BlockSpec((chunk, width), lambda i: (i, 0)),
        ],
        out_specs=[half, half],
        out_shape=[jax.ShapeDtypeStruct((2, vis_rows, HD), BF16)] * 2,
        scratch_shapes=[pltpu.VMEM((vis_rows, width), F32)] * 2,
        compiler_params=pltpu.CompilerParams(dimension_semantics=("arbitrary",)),
        cost_estimate=pl.CostEstimate(
            flops=4 * vis_rows * depth * width,
            bytes_accessed=2 * depth * (vis_rows + 2 * width),
            transcendentals=0,
        ),
    )(side, visual, key_weight, value_weight)
    other = lax.ppermute(send, "xl", [(0, 1), (1, 0)])

    tile_ids = lax.broadcasted_iota(jnp.int32, tile_mask.shape, 1)
    bits = jnp.stack([jnp.sum(jnp.where(tile_ids == tiles[s], tile_mask, 0), axis=1) for s in (0, 1)])
    bits = bits.reshape(2, zs, ys).swapaxes(1, 2).reshape(2, zs * ys)
    pairs = ys * zs // 2
    partials = call(attend_kernel, (pairs, LANES + 16, LANES), [SMEM, SMEM, VMEM, VMEM, VMEM])(
        tiles, bits, gathered.reshape(pairs, 2, piece, LANES), keep, other
    )
    partials = exchange(partials, "y").reshape(ys, zs // 2, LANES + 16, LANES)
    partials = call(join_pairs_kernel, (zs, piece, LANES), [VMEM])(partials)
    partials = exchange(partials, "zh")
    partials = call(join_kernel, (phases, piece, LANES), [VMEM])(partials)
    partials = exchange(partials, ("xh", "xl"))
    return call(finish_kernel, queries.shape, [VMEM])(partials)


def solution(mesh):
    phases, blocks, heads = (mesh.shape[name] for name in ("phase", "blk", "head"))
    fine = jax.sharding.Mesh(
        mesh.devices.reshape(phases // 2, 2, blocks // 8, 8, heads), ("xh", "xl", "zh", "y", "head")
    )
    phase, blk = ("xh", "xl"), ("zh", "y")
    return jax.shard_map(
        per_device,
        mesh=fine,
        in_specs=(
            P(phase + blk, None),
            P(None, "head"),
            P(None, "head"),
            P(blk, "head"),
            P(blk, None),
            P(),
        ),
        out_specs=P(blk, "head"),
        check_vma=False,
    )
```

```python
import math

import jax
import jax.numpy as jnp
from jax import lax
from jax.experimental import pallas as pl
from jax.experimental.pallas import tpu as pltpu
from jax.sharding import PartitionSpec as P

HD = 128
LANES = 128
HIDDEN = -1e30
FLOOR = -1e29
RATE = math.log2(math.e) / math.sqrt(HD)
F32 = jnp.float32
BF16 = jnp.bfloat16
TOGETHER = 2
UNROLL = 2
GRANT = 24 << 20
VMEM = pl.BlockSpec(memory_space=pltpu.VMEM)
SMEM = pl.BlockSpec(memory_space=pltpu.SMEM)


def lane_ids(rows):
    return lax.broadcasted_iota(jnp.int32, (rows, LANES), 1)


def row_ids(rows):
    return lax.broadcasted_iota(jnp.int32, (rows, LANES), 0)


def split3(x):
    first = x.astype(BF16).astype(F32)
    rest = x - first
    second = rest.astype(BF16).astype(F32)
    return first, second, (rest - second).astype(BF16).astype(F32)


def stats_block(top, total):
    parts = split3(top) + split3(total)
    rows = row_ids(16)
    block = jnp.zeros((16, LANES), F32)
    for number, part in enumerate(parts):
        block = jnp.where(rows == number, part, block)
    return block.astype(BF16)


def read_stats(block):
    block = block.astype(F32)
    top = block[0:1] + block[1:2] + block[2:3]
    total = block[3:4] + block[4:5] + block[5:6]
    return top, total


def pack_kernel(side_ref, q_ref, bounds_ref, out_ref):
    rows = q_ref.shape[0]
    width = q_ref.shape[1] // 2
    first = side_ref[0] * width
    blocks = [
        q_ref[:, pl.ds(pl.multiple_of(first + g * HD, HD), HD)] for g in range(width // HD)
    ]
    bounds = bounds_ref[...].astype(F32)
    lanes = lane_ids(rows)
    tail = jnp.zeros((rows, LANES), F32)
    square = (rows, rows)
    diagonal = lax.broadcasted_iota(jnp.int32, square, 0) == lax.broadcasted_iota(
        jnp.int32, square, 1
    )
    for side in range(2):
        row = jnp.broadcast_to(bounds[side:side + 1, :], square)
        value = jnp.sum(jnp.where(diagonal, row, 0.0), axis=1, keepdims=True).astype(jnp.int32)
        pieces = (value >> 9, (value >> 1) & 255, value & 1)
        for number, piece in enumerate(pieces):
            tail = jnp.where(lanes == 3 * side + number, piece.astype(F32), tail)
    blocks.append(tail.astype(BF16))
    packed = jnp.concatenate(blocks, axis=0)
    for copy in range(out_ref.shape[0]):
        out_ref[copy] = packed


def project_kernel(side_ref, x_ref, kw_ref, vw_ref, keep_ref, send_ref, k_acc, v_acc):
    step = pl.program_id(0)

    @pl.when(step == 0)
    def _():
        k_acc[...] = jnp.zeros_like(k_acc)
        v_acc[...] = jnp.zeros_like(v_acc)

    x = x_ref[...]
    k_acc[...] += jnp.dot(x, kw_ref[...], preferred_element_type=F32)
    v_acc[...] += jnp.dot(x, vw_ref[...], preferred_element_type=F32)

    for side in range(2):
        @pl.when((step == pl.num_programs(0) - 1) & (side_ref[0] == side))
        def _():
            for head, out_ref in ((side, keep_ref), (1 - side, send_ref)):
                columns = slice(head * HD, (head + 1) * HD)
                out_ref[0] = k_acc[:, columns].astype(BF16)
                out_ref[1] = v_acc[:, columns].astype(BF16)


def attend_kernel(tiles_ref, bits_ref, q_ref, own_ref, other_ref, out_ref):
    tiles, piece, _ = q_ref.shape
    text = 16
    rows = piece - text
    group = rows // text
    vis = own_ref.shape[1]
    together = TOGETHER
    columns = lax.broadcasted_iota(jnp.int32, (text, vis), 1).astype(F32)

    def step(number, _):
        first = number * together
        edges = []
        for at in range(together):
            digits = q_ref[first + at, rows:, :].astype(F32)
            lower = digits[:, 0:1] * 512 + digits[:, 1:2] * 2 + digits[:, 2:3]
            upper = digits[:, 3:4] * 512 + digits[:, 4:5] * 2 + digits[:, 5:6]
            edges.append((lower, upper))
        queries = jnp.concatenate([q_ref[first + at, :rows, :] for at in range(together)], axis=0)
        scores, tops = [], []
        for source, kv_ref in enumerate((own_ref, other_ref)):
            start = (tiles_ref[source] * vis).astype(F32)
            found = lax.dot_general(
                queries, kv_ref[0], (((1,), (1,)), ((), ())), preferred_element_type=F32
            ).reshape(together, group, text, vis)
            parts = []
            for at in range(together):
                lower, upper = edges[at]
                hidden = (1 - bits_ref[source, first + at]).astype(F32) * 1e7
                visible = (columns >= lower - start + hidden) & (columns < upper - start)
                bias = jnp.where(visible, 0.0, HIDDEN)
                parts.append(found[at] + bias[None])
            masked = jnp.stack(parts).reshape(together * rows, vis)
            scores.append(masked)
            tops.append(jnp.max(masked, axis=1, keepdims=True))
        top = jnp.maximum(jnp.maximum(tops[0], tops[1]), FLOOR)
        total = jnp.zeros((together * rows, 1), F32)
        summed = jnp.zeros((together * rows, HD), F32)
        for masked, kv_ref in zip(scores, (own_ref, other_ref)):
            weights = jnp.exp2((masked - top) * RATE)
            total += jnp.sum(weights, axis=1, keepdims=True)
            summed += jnp.dot(weights.astype(BF16), kv_ref[1], preferred_element_type=F32)
        summed = summed.astype(BF16)
        lanes = lane_ids(LANES)
        for pair in range(together // 2):
            cut = slice(pair * LANES, (pair + 1) * LANES)
            both = jnp.where(lanes == 0, top[cut], jnp.where(lanes == 1, total[cut], 0.0)).T
            both = both[0:8]
            for half in range(2):
                at = 2 * pair + half
                out_ref[first + at, :rows, :] = summed[at * rows:(at + 1) * rows]
                if half:
                    both = pltpu.roll(both, rows, 1)
                out_ref[first + at, rows:, :] = stats_block(both[0:1], both[1:2])
        return 0

    lax.fori_loop(0, tiles // together, step, 0, unroll=UNROLL)


def joined(pieces):
    n = len(pieces)
    rows = pieces[0].shape[0] - 16
    stats = [read_stats(piece[rows:, :]) for piece in pieces]
    tops = jnp.concatenate([top for top, _ in stats], axis=0)
    totals = jnp.concatenate([total for _, total in stats], axis=0)
    top = jnp.max(tops, axis=0, keepdims=True)
    factors = jnp.exp2((tops - top) * RATE)
    total = jnp.sum(factors * totals, axis=0, keepdims=True)
    spread = jnp.concatenate([factors, total, jnp.zeros((LANES - n - 1, LANES), F32)], axis=0).T
    summed = jnp.zeros((rows, LANES), F32)
    for s in range(n):
        summed += spread[:rows, s:s + 1] * pieces[s][:rows, :].astype(F32)
    return top, total, spread[:rows, n:n + 1], summed


def join_kernel(in_ref, out_ref):
    top, total, _, summed = joined([in_ref.at[s] for s in range(in_ref.shape[0])])
    piece = jnp.concatenate([summed.astype(BF16), stats_block(top, total)], axis=0)
    for copy in range(out_ref.shape[0]):
        out_ref[copy] = piece


def finish_kernel(in_ref, out_ref):
    sources = in_ref.shape[0]
    text = out_ref.shape[0]
    for side in range(2):
        _, _, total, summed = joined([in_ref.at[s] for s in range(side, sources, 2)])
        result = (summed / total).astype(BF16)
        group = result.shape[0] // text
        for g in range(group):
            first = (side * group + g) * HD
            out_ref[:, first:first + HD] = result[g * text:(g + 1) * text]


def call(kernel, out, in_specs):
    return pl.pallas_call(
        kernel, out_shape=jax.ShapeDtypeStruct(out, BF16), in_specs=in_specs, out_specs=VMEM,
        compiler_params=pltpu.CompilerParams(vmem_limit_bytes=GRANT),
    )


def per_device(visual, key_weight, value_weight, queries, bounds, tile_mask):
    vis_rows, depth = visual.shape
    width = key_weight.shape[1]
    text = queries.shape[0]
    rows = queries.shape[1] // HD // 2 * text
    piece = rows + text
    zs, ys = lax.axis_size("zh"), lax.axis_size("y")
    phases = lax.axis_size("xh") * 2
    side = lax.axis_index("xl")
    blk = lax.axis_index("zh") * ys + lax.axis_index("y")
    phase = lax.axis_index("xh") * 2 + side
    tiles = jnp.stack([phase * (zs * ys) + blk, (phase ^ 1) * (zs * ys) + blk])
    side = side.reshape(1)

    def exchange(pieces, axis):
        return lax.all_to_all(pieces, axis, 0, 0, tiled=True)

    packed = call(pack_kernel, (zs * ys, piece, LANES), [SMEM, VMEM, VMEM])(side, queries, bounds.T)
    gathered = exchange(packed, ("zh", "y"))

    chunk = 512
    half = pl.BlockSpec((2, vis_rows, HD), lambda i: (0, 0, 0))
    keep, send = pl.pallas_call(
        project_kernel,
        grid=(depth // chunk,),
        in_specs=[
            SMEM,
            pl.BlockSpec((vis_rows, chunk), lambda i: (0, i)),
            pl.BlockSpec((chunk, width), lambda i: (i, 0)),
            pl.BlockSpec((chunk, width), lambda i: (i, 0)),
        ],
        out_specs=[half, half],
        out_shape=[jax.ShapeDtypeStruct((2, vis_rows, HD), BF16)] * 2,
        scratch_shapes=[pltpu.VMEM((vis_rows, width), F32)] * 2,
        compiler_params=pltpu.CompilerParams(dimension_semantics=("arbitrary",), vmem_limit_bytes=62 << 20
        ),
        cost_estimate=pl.CostEstimate(
            flops=4 * vis_rows * depth * width,
            bytes_accessed=2 * depth * (vis_rows + 2 * width),
            transcendentals=0,
        ),
    )(side, visual, key_weight, value_weight)
    other = lax.ppermute(send, "xl", [(0, 1), (1, 0)])

    tile_ids = lax.broadcasted_iota(jnp.int32, tile_mask.shape, 1)
    bits = jnp.sum(jnp.where(tile_ids[None] == tiles[:, None, None], tile_mask[None], 0), axis=2)
    partials = call(attend_kernel, (zs * ys, piece, LANES), [SMEM, SMEM, VMEM, VMEM, VMEM])(
        tiles, bits, gathered, keep, other
    )
    partials = exchange(partials, ("zh", "y"))
    partials = call(join_kernel, (phases, piece, LANES), [VMEM])(partials)
    partials = exchange(partials, ("xh", "xl"))
    return call(finish_kernel, queries.shape, [VMEM])(partials)


def solution(mesh):
    phases, blocks, heads = (mesh.shape[name] for name in ("phase", "blk", "head"))
    fine = jax.sharding.Mesh(
        mesh.devices.reshape(phases // 2, 2, blocks // 8, 8, heads), ("xh", "xl", "zh", "y", "head")
    )
    phase, blk = ("xh", "xl"), ("zh", "y")
    return jax.shard_map(
        per_device,
        mesh=fine,
        in_specs=(
            P(phase + blk, None),
            P(None, "head"),
            P(None, "head"),
            P(blk, "head"),
            P(blk, None),
            P(),
        ),
        out_specs=P(blk, "head"),
        check_vma=False,
    )
```

```python
import math

import jax
import jax.numpy as jnp
from jax import lax
from jax.experimental import pallas as pl
from jax.experimental.pallas import tpu as pltpu
from jax.sharding import PartitionSpec as P

HD = 128
LANES = 128
HIDDEN = -1e30
FLOOR = -1e29
RATE = math.log2(math.e) / math.sqrt(HD)
F32 = jnp.float32
BF16 = jnp.bfloat16
TOGETHER = 4
UNROLL = 2
TAIL = 8
GRANT = 24 << 20
WHOLE = 60 << 20
VMEM = pl.BlockSpec(memory_space=pltpu.VMEM)
SMEM = pl.BlockSpec(memory_space=pltpu.SMEM)


def lane_ids(rows):
    return lax.broadcasted_iota(jnp.int32, (rows, LANES), 1)


def row_ids(rows):
    return lax.broadcasted_iota(jnp.int32, (rows, LANES), 0)


def split3(x):
    first = x.astype(BF16).astype(F32)
    rest = x - first
    second = rest.astype(BF16).astype(F32)
    return first, second, (rest - second).astype(BF16).astype(F32)


def stats_block(top, total):
    parts = split3(top) + split3(total)
    rows = row_ids(TAIL)
    block = jnp.zeros((TAIL, LANES), F32)
    for number, part in enumerate(parts):
        block = jnp.where(rows == number, part, block)
    return block.astype(BF16)


def read_stats(block):
    block = block.astype(F32)
    top = block[0:1] + block[1:2] + block[2:3]
    total = block[3:4] + block[4:5] + block[5:6]
    return top, total


def pack_kernel(side_ref, q_ref, bounds_ref, out_ref):
    rows = q_ref.shape[0]
    width = q_ref.shape[1] // 2
    first = side_ref[0] * width
    blocks = [
        q_ref[:, pl.ds(pl.multiple_of(first + g * HD, HD), HD)] for g in range(width // HD)
    ]
    bounds = bounds_ref[...]
    bounds = jnp.concatenate([bounds, jnp.zeros((2, LANES - rows), jnp.int32)], axis=1)
    numbers = row_ids(TAIL)
    tail = jnp.zeros((TAIL, LANES), F32)
    for side in range(2):
        value = bounds[side:side + 1, :]
        pieces = (value >> 9, (value >> 1) & 255, value & 1)
        for number, digit in enumerate(pieces):
            tail = jnp.where(numbers == 3 * side + number, digit.astype(F32), tail)
    blocks.append(tail.astype(BF16))
    packed = jnp.concatenate(blocks, axis=0)
    for copy in range(out_ref.shape[0]):
        out_ref[copy] = packed


def project_kernel(side_ref, x_ref, kw_ref, vw_ref, keep_ref, send_ref, k_acc, v_acc):
    step = pl.program_id(0)

    @pl.when(step == 0)
    def _():
        k_acc[...] = jnp.zeros_like(k_acc)
        v_acc[...] = jnp.zeros_like(v_acc)

    x = x_ref[...]
    k_acc[...] += jnp.dot(x, kw_ref[...], preferred_element_type=F32)
    v_acc[...] += jnp.dot(x, vw_ref[...], preferred_element_type=F32)

    for side in range(2):
        @pl.when((step == pl.num_programs(0) - 1) & (side_ref[0] == side))
        def _():
            for head, out_ref in ((side, keep_ref), (1 - side, send_ref)):
                columns = slice(head * HD, (head + 1) * HD)
                out_ref[0] = k_acc[:, columns].astype(BF16)
                out_ref[1] = v_acc[:, columns].astype(BF16)


def attend_kernel(tiles_ref, bits_ref, q_ref, own_ref, other_ref, out_ref):
    tiles, piece, _ = q_ref.shape
    text = 16
    rows = piece - TAIL
    group = rows // text
    vis = own_ref.shape[1]
    together = TOGETHER
    columns = lax.broadcasted_iota(jnp.int32, (text, vis), 1).astype(F32)

    def step(number, _):
        first = number * together
        lines = []
        for at in range(together):
            digits = q_ref[first + at, rows:, :].astype(F32)
            lines.append(digits[0:1] * 512 + digits[1:2] * 2 + digits[2:3])
            lines.append(digits[3:4] * 512 + digits[4:5] * 2 + digits[5:6])
        edges = jnp.concatenate(lines, axis=0).T[:text]
        queries = jnp.concatenate([q_ref[first + at, :rows, :] for at in range(together)], axis=0)
        scores, tops = [], []
        for source, kv_ref in enumerate((own_ref, other_ref)):
            start = (tiles_ref[source] * vis).astype(F32)
            found = lax.dot_general(
                queries, kv_ref[0], (((1,), (1,)), ((), ())), preferred_element_type=F32
            ).reshape(together, group, text, vis)
            parts = []
            for at in range(together):
                lower, upper = edges[:, 2 * at:2 * at + 1], edges[:, 2 * at + 1:2 * at + 2]
                hidden = (1 - bits_ref[source, first + at]).astype(F32) * 1e7
                visible = (columns >= lower - start + hidden) & (columns < upper - start)
                bias = jnp.where(visible, 0.0, HIDDEN)
                parts.append(found[at] + bias[None])
            masked = jnp.stack(parts).reshape(together * rows, vis)
            scores.append(masked)
            tops.append(jnp.max(masked, axis=1, keepdims=True))
        top = jnp.maximum(jnp.maximum(tops[0], tops[1]), FLOOR)
        total = jnp.zeros((together * rows, 1), F32)
        summed = jnp.zeros((together * rows, HD), F32)
        for masked, kv_ref in zip(scores, (own_ref, other_ref)):
            weights = jnp.exp2((masked - top) * RATE)
            total += jnp.sum(weights, axis=1, keepdims=True)
            summed += jnp.dot(weights.astype(BF16), kv_ref[1], preferred_element_type=F32)
        summed = summed.astype(BF16)
        lanes = lane_ids(LANES)
        for pair in range(together // 2):
            cut = slice(pair * LANES, (pair + 1) * LANES)
            both = jnp.where(lanes == 0, top[cut], jnp.where(lanes == 1, total[cut], 0.0)).T
            both = both[0:8]
            for half in range(2):
                at = 2 * pair + half
                out_ref[first + at, :rows, :] = summed[at * rows:(at + 1) * rows]
                if half:
                    both = pltpu.roll(both, rows, 1)
                out_ref[first + at, rows:, :] = stats_block(both[0:1], both[1:2])
        return 0

    lax.fori_loop(0, tiles // together, step, 0, unroll=UNROLL)


def joined(pieces):
    n = len(pieces)
    rows = pieces[0].shape[0] - TAIL
    stats = [read_stats(piece[rows:, :]) for piece in pieces]
    tops = jnp.concatenate([top for top, _ in stats], axis=0)
    totals = jnp.concatenate([total for _, total in stats], axis=0)
    top = jnp.max(tops, axis=0, keepdims=True)
    factors = jnp.exp2((tops - top) * RATE)
    total = jnp.sum(factors * totals, axis=0, keepdims=True)
    spread = jnp.concatenate([factors, total, jnp.zeros((LANES - n - 1, LANES), F32)], axis=0).T
    summed = jnp.zeros((rows, LANES), F32)
    for s in range(n):
        summed += spread[:rows, s:s + 1] * pieces[s][:rows, :].astype(F32)
    return top, total, spread[:rows, n:n + 1], summed


def join_kernel(in_ref, out_ref):
    top, total, _, summed = joined([in_ref.at[s] for s in range(in_ref.shape[0])])
    piece = jnp.concatenate([summed.astype(BF16), stats_block(top, total)], axis=0)
    for copy in range(out_ref.shape[0]):
        out_ref[copy] = piece


def finish_kernel(in_ref, out_ref):
    sources = in_ref.shape[0]
    text = out_ref.shape[0]
    for side in range(2):
        _, _, total, summed = joined([in_ref.at[s] for s in range(side, sources, 2)])
        result = (summed / total).astype(BF16)
        group = result.shape[0] // text
        for g in range(group):
            first = (side * group + g) * HD
            out_ref[:, first:first + HD] = result[g * text:(g + 1) * text]


def call(kernel, out, in_specs, grant=GRANT):
    return pl.pallas_call(
        kernel, out_shape=jax.ShapeDtypeStruct(out, BF16), in_specs=in_specs, out_specs=VMEM,
        compiler_params=pltpu.CompilerParams(vmem_limit_bytes=grant),
    )


def per_device(visual, key_weight, value_weight, queries, bounds, tile_mask):
    vis_rows, depth = visual.shape
    width = key_weight.shape[1]
    text = queries.shape[0]
    rows = queries.shape[1] // HD // 2 * text
    piece = rows + TAIL
    zs, ys = lax.axis_size("zh"), lax.axis_size("y")
    phases = lax.axis_size("xh") * 2
    side = lax.axis_index("xl")
    blk = lax.axis_index("zh") * ys + lax.axis_index("y")
    phase = lax.axis_index("xh") * 2 + side
    tiles = jnp.stack([phase * (zs * ys) + blk, (phase ^ 1) * (zs * ys) + blk])
    side = side.reshape(1)

    def exchange(pieces, axis):
        return lax.all_to_all(pieces, axis, 0, 0, tiled=True)

    packed = call(pack_kernel, (zs * ys, piece, LANES), [SMEM, VMEM, VMEM], WHOLE)(
        side, queries, bounds.T
    )
    gathered = exchange(packed, ("zh", "y"))

    chunk = 512
    half = pl.BlockSpec((2, vis_rows, HD), lambda i: (0, 0, 0))
    keep, send = pl.pallas_call(
        project_kernel,
        grid=(depth // chunk,),
        in_specs=[
            SMEM,
            pl.BlockSpec((vis_rows, chunk), lambda i: (0, i)),
            pl.BlockSpec((chunk, width), lambda i: (i, 0)),
            pl.BlockSpec((chunk, width), lambda i: (i, 0)),
        ],
        out_specs=[half, half],
        out_shape=[jax.ShapeDtypeStruct((2, vis_rows, HD), BF16)] * 2,
        scratch_shapes=[pltpu.VMEM((vis_rows, width), F32)] * 2,
        compiler_params=pltpu.CompilerParams(dimension_semantics=("arbitrary",), vmem_limit_bytes=WHOLE
        ),
        cost_estimate=pl.CostEstimate(
            flops=4 * vis_rows * depth * width,
            bytes_accessed=2 * depth * (vis_rows + 2 * width),
            transcendentals=0,
        ),
    )(side, visual, key_weight, value_weight)
    other = lax.ppermute(send, "xl", [(0, 1), (1, 0)])

    tile_ids = lax.broadcasted_iota(jnp.int32, tile_mask.shape, 1)
    bits = jnp.sum(jnp.where(tile_ids[None] == tiles[:, None, None], tile_mask[None], 0), axis=2)
    partials = call(attend_kernel, (zs * ys, piece, LANES), [SMEM, SMEM, VMEM, VMEM, VMEM])(
        tiles, bits, gathered, keep, other
    )
    partials = exchange(partials, ("zh", "y"))
    partials = call(join_kernel, (phases, piece, LANES), [VMEM])(partials)
    partials = exchange(partials, ("xh", "xl"))
    return call(finish_kernel, queries.shape, [VMEM])(partials)


def solution(mesh):
    phases, blocks, heads = (mesh.shape[name] for name in ("phase", "blk", "head"))
    fine = jax.sharding.Mesh(
        mesh.devices.reshape(phases // 2, 2, blocks // 8, 8, heads), ("xh", "xl", "zh", "y", "head")
    )
    phase, blk = ("xh", "xl"), ("zh", "y")
    return jax.shard_map(
        per_device,
        mesh=fine,
        in_specs=(
            P(phase + blk, None),
            P(None, "head"),
            P(None, "head"),
            P(blk, "head"),
            P(blk, None),
            P(),
        ),
        out_specs=P(blk, "head"),
        check_vma=False,
    )
```

```python
import math

import jax
import jax.numpy as jnp
from jax import lax
from jax.experimental import pallas as pl
from jax.experimental.pallas import tpu as pltpu
from jax.sharding import PartitionSpec as P

HD = 128
LANES = 128
HIDDEN = -1e30
FLOOR = -1e29
RATE = math.log2(math.e) / math.sqrt(HD)
F32 = jnp.float32
BF16 = jnp.bfloat16
TOGETHER = 4
UNROLL = 2
TAIL = 8
GRANT = 24 << 20
WHOLE = 60 << 20
ROOM = 52 << 20
CHUNK = 512
VMEM = pl.BlockSpec(memory_space=pltpu.VMEM)
SMEM = pl.BlockSpec(memory_space=pltpu.SMEM)


def lane_ids(rows):
    return lax.broadcasted_iota(jnp.int32, (rows, LANES), 1)


def row_ids(rows):
    return lax.broadcasted_iota(jnp.int32, (rows, LANES), 0)


def split3(x):
    first = x.astype(BF16).astype(F32)
    rest = x - first
    second = rest.astype(BF16).astype(F32)
    return first, second, (rest - second).astype(BF16).astype(F32)


def stats_block(top, total):
    parts = split3(top) + split3(total)
    rows = row_ids(TAIL)
    block = jnp.zeros((TAIL, LANES), F32)
    for number, part in enumerate(parts):
        block = jnp.where(rows == number, part, block)
    return block.astype(BF16)


def read_stats(block):
    block = block.astype(F32)
    top = block[0:1] + block[1:2] + block[2:3]
    total = block[3:4] + block[4:5] + block[5:6]
    return top, total


def pack_kernel(side_ref, q_ref, bounds_ref, out_ref):
    rows = q_ref.shape[0]
    width = q_ref.shape[1] // 2
    first = side_ref[0] * width
    blocks = [
        q_ref[:, pl.ds(pl.multiple_of(first + g * HD, HD), HD)] for g in range(width // HD)
    ]
    bounds = bounds_ref[...]
    bounds = jnp.concatenate([bounds, jnp.zeros((2, LANES - rows), jnp.int32)], axis=1)
    numbers = row_ids(TAIL)
    tail = jnp.zeros((TAIL, LANES), F32)
    for side in range(2):
        value = bounds[side:side + 1, :]
        pieces = (value >> 9, (value >> 1) & 255, value & 1)
        for number, digit in enumerate(pieces):
            tail = jnp.where(numbers == 3 * side + number, digit.astype(F32), tail)
    blocks.append(tail.astype(BF16))
    packed = jnp.concatenate(blocks, axis=0)
    for copy in range(out_ref.shape[0]):
        out_ref[copy] = packed


def project_kernel(side_ref, x_ref, kw_ref, vw_ref, keep_ref, send_ref, x_buf, kw_buf, vw_buf, k_acc, v_acc, sems):
    chunks, _, chunk = x_buf.shape
    copies = []
    for c in range(chunks):
        span = slice(c * chunk, (c + 1) * chunk)
        copies.append((
            pltpu.make_async_copy(x_ref.at[:, span], x_buf.at[c], sems.at[c, 0]),
            pltpu.make_async_copy(kw_ref.at[span, :], kw_buf.at[c], sems.at[c, 1]),
            pltpu.make_async_copy(vw_ref.at[span, :], vw_buf.at[c], sems.at[c, 2]),
        ))
    for group in copies:
        for copy in group:
            copy.start()
    for c, group in enumerate(copies):
        for copy in group:
            copy.wait()
        x = x_buf[c]
        k_part = jnp.dot(x, kw_buf[c], preferred_element_type=F32)
        v_part = jnp.dot(x, vw_buf[c], preferred_element_type=F32)
        if c:
            k_part += k_acc[...]
            v_part += v_acc[...]
        k_acc[...] = k_part
        v_acc[...] = v_part
    for side in range(2):
        @pl.when(side_ref[0] == side)
        def _():
            for head, out_ref in ((side, keep_ref), (1 - side, send_ref)):
                columns = slice(head * HD, (head + 1) * HD)
                out_ref[0] = k_acc[:, columns].astype(BF16)
                out_ref[1] = v_acc[:, columns].astype(BF16)


def attend_kernel(tiles_ref, bits_ref, q_ref, own_ref, other_ref, out_ref):
    tiles, piece, _ = q_ref.shape
    text = 16
    rows = piece - TAIL
    group = rows // text
    vis = own_ref.shape[1]
    together = TOGETHER
    columns = lax.broadcasted_iota(jnp.int32, (text, vis), 1).astype(F32)

    def step(number, _):
        first = number * together
        lines = []
        for at in range(together):
            digits = q_ref[first + at, rows:, :].astype(F32)
            lines.append(digits[0:1] * 512 + digits[1:2] * 2 + digits[2:3])
            lines.append(digits[3:4] * 512 + digits[4:5] * 2 + digits[5:6])
        edges = jnp.concatenate(lines, axis=0).T[:text]
        queries = jnp.concatenate([q_ref[first + at, :rows, :] for at in range(together)], axis=0)
        scores, tops = [], []
        for source, kv_ref in enumerate((own_ref, other_ref)):
            start = (tiles_ref[source] * vis).astype(F32)
            found = lax.dot_general(
                queries, kv_ref[0], (((1,), (1,)), ((), ())), preferred_element_type=F32
            ).reshape(together, group, text, vis)
            parts = []
            for at in range(together):
                lower, upper = edges[:, 2 * at:2 * at + 1], edges[:, 2 * at + 1:2 * at + 2]
                hidden = (1 - bits_ref[source, first + at]).astype(F32) * 1e7
                visible = (columns >= lower - start + hidden) & (columns < upper - start)
                bias = jnp.where(visible, 0.0, HIDDEN)
                parts.append(found[at] + bias[None])
            masked = jnp.stack(parts).reshape(together * rows, vis)
            scores.append(masked)
            tops.append(jnp.max(masked, axis=1, keepdims=True))
        top = jnp.maximum(jnp.maximum(tops[0], tops[1]), FLOOR)
        total = jnp.zeros((together * rows, 1), F32)
        summed = jnp.zeros((together * rows, HD), F32)
        for masked, kv_ref in zip(scores, (own_ref, other_ref)):
            weights = jnp.exp2((masked - top) * RATE)
            total += jnp.sum(weights, axis=1, keepdims=True)
            summed += jnp.dot(weights.astype(BF16), kv_ref[1], preferred_element_type=F32)
        summed = summed.astype(BF16)
        lanes = lane_ids(LANES)
        for pair in range(together // 2):
            cut = slice(pair * LANES, (pair + 1) * LANES)
            both = jnp.where(lanes == 0, top[cut], jnp.where(lanes == 1, total[cut], 0.0)).T
            both = both[0:8]
            for half in range(2):
                at = 2 * pair + half
                out_ref[first + at, :rows, :] = summed[at * rows:(at + 1) * rows]
                if half:
                    both = pltpu.roll(both, rows, 1)
                out_ref[first + at, rows:, :] = stats_block(both[0:1], both[1:2])
        return 0

    lax.fori_loop(0, tiles // together, step, 0, unroll=UNROLL)


def joined(pieces):
    n = len(pieces)
    rows = pieces[0].shape[0] - TAIL
    stats = [read_stats(piece[rows:, :]) for piece in pieces]
    tops = jnp.concatenate([top for top, _ in stats], axis=0)
    totals = jnp.concatenate([total for _, total in stats], axis=0)
    top = jnp.max(tops, axis=0, keepdims=True)
    factors = jnp.exp2((tops - top) * RATE)
    total = jnp.sum(factors * totals, axis=0, keepdims=True)
    spread = jnp.concatenate([factors, total, jnp.zeros((LANES - n - 1, LANES), F32)], axis=0).T
    summed = jnp.zeros((rows, LANES), F32)
    for s in range(n):
        summed += spread[:rows, s:s + 1] * pieces[s][:rows, :].astype(F32)
    return top, total, spread[:rows, n:n + 1], summed


def join_kernel(in_ref, out_ref):
    top, total, _, summed = joined([in_ref.at[s] for s in range(in_ref.shape[0])])
    piece = jnp.concatenate([summed.astype(BF16), stats_block(top, total)], axis=0)
    for copy in range(out_ref.shape[0]):
        out_ref[copy] = piece


def finish_kernel(in_ref, out_ref):
    sources = in_ref.shape[0]
    text = out_ref.shape[0]
    for side in range(2):
        _, _, total, summed = joined([in_ref.at[s] for s in range(side, sources, 2)])
        result = (summed / total).astype(BF16)
        group = result.shape[0] // text
        for g in range(group):
            first = (side * group + g) * HD
            out_ref[:, first:first + HD] = result[g * text:(g + 1) * text]


def call(kernel, out, in_specs, grant=GRANT):
    return pl.pallas_call(
        kernel, out_shape=jax.ShapeDtypeStruct(out, BF16), in_specs=in_specs, out_specs=VMEM,
        compiler_params=pltpu.CompilerParams(vmem_limit_bytes=grant),
    )


def project(side, visual, key_weight, value_weight):
    vis_rows, depth = visual.shape
    width = key_weight.shape[1]
    chunks, chunk = depth // CHUNK, CHUNK
    anywhere = pl.BlockSpec(memory_space=pl.ANY)
    return pl.pallas_call(
        project_kernel,
        in_specs=[SMEM, anywhere, anywhere, anywhere],
        out_specs=[VMEM, VMEM],
        out_shape=[jax.ShapeDtypeStruct((2, vis_rows, HD), BF16)] * 2,
        scratch_shapes=[
            pltpu.VMEM((chunks, vis_rows, chunk), BF16),
            pltpu.VMEM((chunks, chunk, width), BF16),
            pltpu.VMEM((chunks, chunk, width), BF16),
            pltpu.VMEM((vis_rows, width), F32),
            pltpu.VMEM((vis_rows, width), F32),
            pltpu.SemaphoreType.DMA((chunks, 3)),
        ],
        compiler_params=pltpu.CompilerParams(vmem_limit_bytes=ROOM),
        cost_estimate=pl.CostEstimate(
            flops=4 * vis_rows * depth * width,
            bytes_accessed=2 * depth * (vis_rows + 2 * width),
            transcendentals=0,
        ),
    )(side, visual, key_weight, value_weight)


def per_device(visual, key_weight, value_weight, queries, bounds, tile_mask):
    text = queries.shape[0]
    rows = queries.shape[1] // HD // 2 * text
    piece = rows + TAIL
    zs, ys = lax.axis_size("zh"), lax.axis_size("y")
    phases = lax.axis_size("xh") * 2
    side = lax.axis_index("xl")
    blk = lax.axis_index("zh") * ys + lax.axis_index("y")
    phase = lax.axis_index("xh") * 2 + side
    tiles = jnp.stack([phase * (zs * ys) + blk, (phase ^ 1) * (zs * ys) + blk])
    side = side.reshape(1)

    def exchange(pieces, axis):
        return lax.all_to_all(pieces, axis, 0, 0, tiled=True)

    packed = call(pack_kernel, (zs * ys, piece, LANES), [SMEM, VMEM, VMEM], WHOLE)(
        side, queries, bounds.T
    )
    gathered = exchange(packed, ("zh", "y"))

    keep, send = project(side, visual, key_weight, value_weight)
    other = lax.ppermute(send, "xl", [(0, 1), (1, 0)])

    tile_ids = lax.broadcasted_iota(jnp.int32, tile_mask.shape, 1)
    bits = jnp.sum(jnp.where(tile_ids[None] == tiles[:, None, None], tile_mask[None], 0), axis=2)
    partials = call(attend_kernel, (zs * ys, piece, LANES), [SMEM, SMEM, VMEM, VMEM, VMEM])(
        tiles, bits, gathered, keep, other
    )
    partials = exchange(partials, ("zh", "y"))
    partials = call(join_kernel, (phases, piece, LANES), [VMEM])(partials)
    partials = exchange(partials, ("xh", "xl"))
    return call(finish_kernel, queries.shape, [VMEM])(partials)


def solution(mesh):
    phases, blocks, heads = (mesh.shape[name] for name in ("phase", "blk", "head"))
    fine = jax.sharding.Mesh(
        mesh.devices.reshape(phases // 2, 2, blocks // 8, 8, heads), ("xh", "xl", "zh", "y", "head")
    )
    phase, blk = ("xh", "xl"), ("zh", "y")
    return jax.shard_map(
        per_device,
        mesh=fine,
        in_specs=(
            P(phase + blk, None),
            P(None, "head"),
            P(None, "head"),
            P(blk, "head"),
            P(blk, None),
            P(),
        ),
        out_specs=P(blk, "head"),
        check_vma=False,
    )
```

```python
import math

import jax
import jax.numpy as jnp
from jax import lax
from jax.experimental import pallas as pl
from jax.experimental.pallas import tpu as pltpu
from jax.sharding import PartitionSpec as P

HD = 128
LANES = 128
HIDDEN = -1e30
FLOOR = -1e29
RATE = math.log2(math.e) / math.sqrt(HD)
F32 = jnp.float32
BF16 = jnp.bfloat16
TOGETHER = 8
UNROLL = 1
TAIL = 8
TEXT_PART = 8
GRANT = 24 << 20
WHOLE = 60 << 20
ROOM = 52 << 20
CHUNK = 512
VMEM = pl.BlockSpec(memory_space=pltpu.VMEM)
SMEM = pl.BlockSpec(memory_space=pltpu.SMEM)


def lane_ids(rows):
    return lax.broadcasted_iota(jnp.int32, (rows, LANES), 1)


def row_ids(rows):
    return lax.broadcasted_iota(jnp.int32, (rows, LANES), 0)


def split3(x):
    first = x.astype(BF16).astype(F32)
    rest = x - first
    second = rest.astype(BF16).astype(F32)
    return first, second, (rest - second).astype(BF16).astype(F32)


def stats_block(top, total):
    parts = split3(top) + split3(total)
    rows = row_ids(TAIL)
    block = jnp.zeros((TAIL, LANES), F32)
    for number, part in enumerate(parts):
        block = jnp.where(rows == number, part, block)
    return block.astype(BF16)


def read_stats(block):
    block = block.astype(F32)
    top = block[0:1] + block[1:2] + block[2:3]
    total = block[3:4] + block[4:5] + block[5:6]
    return top, total


def pack_kernel(side_ref, q_ref, bounds_ref, out_ref):
    rows = q_ref.shape[0]
    width = q_ref.shape[1] // 2
    first = side_ref[0] * width
    heads = [
        q_ref[:, pl.ds(pl.multiple_of(first + g * HD, HD), HD)].astype(F32)
        for g in range(width // HD)
    ]
    bounds = bounds_ref[...]
    bounds = jnp.concatenate([bounds, jnp.zeros((2, LANES - rows), jnp.int32)], axis=1)
    numbers = row_ids(TAIL)
    tail = jnp.zeros((TAIL, LANES), F32)
    for side in range(2):
        value = bounds[side:side + 1, :]
        pieces = (value >> 9, (value >> 1) & 255, value & 1)
        for number, digit in enumerate(pieces):
            tail = jnp.where(numbers == 3 * side + number, digit.astype(F32), tail)
    part = rows // 2
    packed = []
    for half in range(2):
        blocks = [head[half * part:(half + 1) * part] for head in heads]
        blocks.append(pltpu.roll(tail, LANES - part, 1) if half else tail)
        packed.append(jnp.concatenate(blocks, axis=0).astype(BF16))
    for copy in range(out_ref.shape[0]):
        out_ref[copy] = packed[copy % 2]


def project_kernel(side_ref, x_ref, kw_ref, vw_ref, keep_ref, send_ref, x_buf, kw_buf, vw_buf, k_acc, v_acc, sems):
    chunks, _, chunk = x_buf.shape
    copies = []
    for c in range(chunks):
        span = slice(c * chunk, (c + 1) * chunk)
        copies.append((
            pltpu.make_async_copy(x_ref.at[:, span], x_buf.at[c], sems.at[c, 0]),
            pltpu.make_async_copy(kw_ref.at[span, :], kw_buf.at[c], sems.at[c, 1]),
            pltpu.make_async_copy(vw_ref.at[span, :], vw_buf.at[c], sems.at[c, 2]),
        ))
    for group in copies:
        for copy in group:
            copy.start()
    for c, group in enumerate(copies):
        for copy in group:
            copy.wait()
        x = x_buf[c]
        k_part = jnp.dot(x, kw_buf[c], preferred_element_type=F32)
        v_part = jnp.dot(x, vw_buf[c], preferred_element_type=F32)
        if c:
            k_part += k_acc[...]
            v_part += v_acc[...]
        k_acc[...] = k_part
        v_acc[...] = v_part
    for side in range(2):
        @pl.when(side_ref[0] == side)
        def _():
            for head, out_ref in ((side, keep_ref), (1 - side, send_ref)):
                columns = slice(head * HD, (head + 1) * HD)
                out_ref[0] = k_acc[:, columns].astype(BF16)
                out_ref[1] = v_acc[:, columns].astype(BF16)


def attend_kernel(tiles_ref, bits_ref, q_ref, *refs):
    sources, out_ref = refs[:-1], refs[-1]
    tiles, piece, _ = q_ref.shape
    text = TEXT_PART
    rows = piece - TAIL
    group = rows // text
    vis = sources[0].shape[1]
    together = TOGETHER
    columns = lax.broadcasted_iota(jnp.int32, (text, vis), 1).astype(F32)

    def step(number, _):
        first = number * together
        lines = []
        for at in range(together):
            digits = q_ref[first + at, rows:, :].astype(F32)
            lines.append(digits[0:1] * 512 + digits[1:2] * 2 + digits[2:3])
            lines.append(digits[3:4] * 512 + digits[4:5] * 2 + digits[5:6])
        edges = jnp.concatenate(lines, axis=0).T[:text]
        queries = jnp.concatenate([q_ref[first + at, :rows, :] for at in range(together)], axis=0)
        scores, tops = [], []
        for source, kv_ref in enumerate(sources):
            start = (tiles_ref[source] * vis).astype(F32)
            found = lax.dot_general(
                queries, kv_ref[0], (((1,), (1,)), ((), ())), preferred_element_type=F32
            ).reshape(together, group, text, vis)
            parts = []
            for at in range(together):
                lower, upper = edges[:, 2 * at:2 * at + 1], edges[:, 2 * at + 1:2 * at + 2]
                hidden = (1 - bits_ref[source, first + at]).astype(F32) * 1e7
                visible = (columns >= lower - start + hidden) & (columns < upper - start)
                bias = jnp.where(visible, 0.0, HIDDEN)
                parts.append(found[at] + bias[None])
            masked = jnp.stack(parts).reshape(together * rows, vis)
            scores.append(masked)
            tops.append(jnp.max(masked, axis=1, keepdims=True))
        top = jnp.full((together * rows, 1), FLOOR, F32)
        for one in tops:
            top = jnp.maximum(top, one)
        total = jnp.zeros((together * rows, 1), F32)
        summed = jnp.zeros((together * rows, HD), F32)
        for masked, kv_ref in zip(scores, sources):
            weights = jnp.exp2((masked - top) * RATE)
            total += jnp.sum(weights, axis=1, keepdims=True)
            summed += jnp.dot(weights.astype(BF16), kv_ref[1], preferred_element_type=F32)
        summed = summed.astype(BF16)
        lanes = lane_ids(LANES)
        per = LANES // rows
        for block in range(together // per):
            cut = slice(block * LANES, (block + 1) * LANES)
            both = jnp.where(lanes == 0, top[cut], jnp.where(lanes == 1, total[cut], 0.0)).T
            both = both[0:8]
            for within in range(per):
                at = per * block + within
                out_ref[first + at, :rows, :] = summed[at * rows:(at + 1) * rows]
                mine = pltpu.roll(both, LANES - rows * within, 1) if within else both
                out_ref[first + at, rows:, :] = stats_block(mine[0:1], mine[1:2])
        return 0

    lax.fori_loop(0, tiles // together, step, 0, unroll=UNROLL)


def joined(pieces):
    n = len(pieces)
    rows = pieces[0].shape[0] - TAIL
    stats = [read_stats(piece[rows:, :]) for piece in pieces]
    tops = jnp.concatenate([top for top, _ in stats], axis=0)
    totals = jnp.concatenate([total for _, total in stats], axis=0)
    top = jnp.max(tops, axis=0, keepdims=True)
    factors = jnp.exp2((tops - top) * RATE)
    total = jnp.sum(factors * totals, axis=0, keepdims=True)
    spread = jnp.concatenate([factors, total, jnp.zeros((LANES - n - 1, LANES), F32)], axis=0).T
    summed = jnp.zeros((rows, LANES), F32)
    for s in range(n):
        summed += spread[:rows, s:s + 1] * pieces[s][:rows, :].astype(F32)
    return top, total, spread[:rows, n:n + 1], summed


def join_kernel(in_ref, out_ref):
    n = in_ref.shape[0]
    first, second = (joined([in_ref.at[s] for s in range(half, n, 2)]) for half in range(2))
    rows = first[3].shape[0]
    lanes = lane_ids(1)
    top, total = (
        jnp.where(lanes < rows, first[i], pltpu.roll(second[i], rows, 1)) for i in range(2)
    )
    piece = jnp.concatenate(
        [first[3].astype(BF16), second[3].astype(BF16), stats_block(top, total)], axis=0
    )
    for copy in range(out_ref.shape[0]):
        out_ref[copy] = piece


def finish_kernel(in_ref, out_ref):
    sources = in_ref.shape[0]
    part = TEXT_PART
    for side in range(2):
        _, _, total, summed = joined([in_ref.at[s] for s in range(side, sources, 2)])
        result = summed / total
        rows = result.shape[0] // 2
        group = rows // part
        for g in range(group):
            first = (side * group + g) * HD
            block = [result[h * rows + g * part:h * rows + (g + 1) * part] for h in range(2)]
            out_ref[:, first:first + HD] = jnp.concatenate(block, axis=0).astype(BF16)


def call(kernel, out, in_specs, grant=GRANT):
    return pl.pallas_call(
        kernel, out_shape=jax.ShapeDtypeStruct(out, BF16), in_specs=in_specs, out_specs=VMEM,
        compiler_params=pltpu.CompilerParams(vmem_limit_bytes=grant),
    )


def project(side, visual, key_weight, value_weight):
    vis_rows, depth = visual.shape
    width = key_weight.shape[1]
    chunks, chunk = depth // CHUNK, CHUNK
    anywhere = pl.BlockSpec(memory_space=pl.ANY)
    return pl.pallas_call(
        project_kernel,
        in_specs=[SMEM, anywhere, anywhere, anywhere],
        out_specs=[VMEM, VMEM],
        out_shape=[jax.ShapeDtypeStruct((2, vis_rows, HD), BF16)] * 2,
        scratch_shapes=[
            pltpu.VMEM((chunks, vis_rows, chunk), BF16),
            pltpu.VMEM((chunks, chunk, width), BF16),
            pltpu.VMEM((chunks, chunk, width), BF16),
            pltpu.VMEM((vis_rows, width), F32),
            pltpu.VMEM((vis_rows, width), F32),
            pltpu.SemaphoreType.DMA((chunks, 3)),
        ],
        compiler_params=pltpu.CompilerParams(vmem_limit_bytes=ROOM),
        cost_estimate=pl.CostEstimate(
            flops=4 * vis_rows * depth * width,
            bytes_accessed=2 * depth * (vis_rows + 2 * width),
            transcendentals=0,
        ),
    )(side, visual, key_weight, value_weight)


def per_device(visual, key_weight, value_weight, queries, bounds, tile_mask):
    text = queries.shape[0]
    heads = queries.shape[1] // HD // 2
    zs, ys = lax.axis_size("zh"), lax.axis_size("yh") * 2
    phases = lax.axis_size("xh") * 2
    side = lax.axis_index("xl")
    blk = lax.axis_index("zh") * ys + lax.axis_index("yh") * 2 + lax.axis_index("yl")
    phase = lax.axis_index("xh") * 2 + side
    tiles = jnp.stack([p * (zs * ys) + b for b in (blk, blk ^ 1) for p in (phase, phase ^ 1)])
    side = side.reshape(1)

    def exchange(pieces, axis):
        return lax.all_to_all(pieces, axis, 0, 0, tiled=True)

    half = heads * text // 2 + TAIL
    whole = heads * text + TAIL
    blocks = ("zh", "yh", "yl")
    packed = call(pack_kernel, (zs * ys, half, LANES), [SMEM, VMEM, VMEM], WHOLE)(
        side, queries, bounds.T
    )
    gathered = exchange(packed, blocks)

    keep, send = project(side, visual, key_weight, value_weight)
    swap = [(0, 1), (1, 0)]
    beside = lax.ppermute(send, "xl", swap)
    across = lax.ppermute(send, ("xl", "yl"), [(0, 3), (1, 2), (2, 1), (3, 0)])
    above = lax.ppermute(keep, "yl", swap)

    tile_ids = lax.broadcasted_iota(jnp.int32, tile_mask.shape, 1)
    bits = jnp.sum(jnp.where(tile_ids[None] == tiles[:, None, None], tile_mask[None], 0), axis=2)
    partials = call(attend_kernel, (zs * ys, half, LANES), [SMEM, SMEM] + [VMEM] * 5)(
        tiles, bits, gathered, keep, beside, above, across
    )
    partials = exchange(partials, blocks)
    partials = call(join_kernel, (phases, whole, LANES), [VMEM])(partials)
    partials = exchange(partials, ("xh", "xl"))
    return call(finish_kernel, queries.shape, [VMEM])(partials)


def solution(mesh):
    phases, blocks, heads = (mesh.shape[name] for name in ("phase", "blk", "head"))
    fine = jax.sharding.Mesh(
        mesh.devices.reshape(phases // 2, 2, blocks // 8, 4, 2, heads),
        ("xh", "xl", "zh", "yh", "yl", "head"),
    )
    phase, blk = ("xh", "xl"), ("zh", "yh", "yl")
    return jax.shard_map(
        per_device,
        mesh=fine,
        in_specs=(
            P(phase + blk, None),
            P(None, "head"),
            P(None, "head"),
            P(blk, "head"),
            P(blk, None),
            P(),
        ),
        out_specs=P(blk, "head"),
        check_vma=False,
    )
```

```python
import math

import jax
import jax.numpy as jnp
from jax import lax
from jax.experimental import pallas as pl
from jax.experimental.pallas import tpu as pltpu
from jax.sharding import PartitionSpec as P

HD = 128
LANES = 128
HIDDEN = -1e30
FLOOR = -1e29
RATE = math.log2(math.e) / math.sqrt(HD)
F32 = jnp.float32
BF16 = jnp.bfloat16
TOGETHER = 4
UNROLL = 4
TAIL = 8
GRANT = 24 << 20
WHOLE = 60 << 20
ROOM = 52 << 20
CHUNK = 512
VMEM = pl.BlockSpec(memory_space=pltpu.VMEM)
SMEM = pl.BlockSpec(memory_space=pltpu.SMEM)


def lane_ids(rows):
    return lax.broadcasted_iota(jnp.int32, (rows, LANES), 1)


def row_ids(rows):
    return lax.broadcasted_iota(jnp.int32, (rows, LANES), 0)


def split3(x):
    first = x.astype(BF16).astype(F32)
    rest = x - first
    second = rest.astype(BF16).astype(F32)
    return first, second, (rest - second).astype(BF16).astype(F32)


def stats_block(top, total):
    parts = split3(top) + split3(total)
    rows = row_ids(TAIL)
    block = jnp.zeros((TAIL, LANES), F32)
    for number, part in enumerate(parts):
        block = jnp.where(rows == number, part, block)
    return block.astype(BF16)


def read_stats(block):
    block = block.astype(F32)
    top = block[0:1] + block[1:2] + block[2:3]
    total = block[3:4] + block[4:5] + block[5:6]
    return top, total


def pack_kernel(side_ref, q_ref, bounds_ref, out_ref, packed, sems):
    rows = q_ref.shape[0]
    width = q_ref.shape[1] // 2
    first = side_ref[0] * width
    blocks = [
        q_ref[:, pl.ds(pl.multiple_of(first + g * HD, HD), HD)] for g in range(width // HD)
    ]
    bounds = bounds_ref[...]
    bounds = jnp.concatenate([bounds, jnp.zeros((2, LANES - rows), jnp.int32)], axis=1)
    numbers = row_ids(TAIL)
    tail = jnp.zeros((TAIL, LANES), F32)
    for side in range(2):
        value = bounds[side:side + 1, :]
        pieces = (value >> 9, (value >> 1) & 255, value & 1)
        for number, digit in enumerate(pieces):
            tail = jnp.where(numbers == 3 * side + number, digit.astype(F32), tail)
    blocks.append(tail.astype(BF16))
    packed[...] = jnp.concatenate(blocks, axis=0)
    copies = [
        pltpu.make_async_copy(packed, out_ref.at[copy], sems.at[copy])
        for copy in range(out_ref.shape[0])
    ]
    for copy in copies:
        copy.start()
    for copy in copies:
        copy.wait()


def project_kernel(side_ref, x_ref, kw_ref, vw_ref, keep_ref, send_ref, x_buf, kw_buf, vw_buf, k_acc, v_acc, sems):
    chunks, _, chunk = x_buf.shape
    copies = []
    for c in range(chunks):
        span = slice(c * chunk, (c + 1) * chunk)
        copies.append((
            pltpu.make_async_copy(x_ref.at[:, span], x_buf.at[c], sems.at[c, 0]),
            pltpu.make_async_copy(kw_ref.at[span, :], kw_buf.at[c], sems.at[c, 1]),
            pltpu.make_async_copy(vw_ref.at[span, :], vw_buf.at[c], sems.at[c, 2]),
        ))
    for group in copies:
        for copy in group:
            copy.start()
    for c, group in enumerate(copies):
        for copy in group:
            copy.wait()
        x = x_buf[c]
        k_part = jnp.dot(x, kw_buf[c], preferred_element_type=F32)
        v_part = jnp.dot(x, vw_buf[c], preferred_element_type=F32)
        if c:
            k_part += k_acc[...]
            v_part += v_acc[...]
        k_acc[...] = k_part
        v_acc[...] = v_part
    for side in range(2):
        @pl.when(side_ref[0] == side)
        def _():
            for head, out_ref in ((side, keep_ref), (1 - side, send_ref)):
                columns = slice(head * HD, (head + 1) * HD)
                out_ref[0] = k_acc[:, columns].astype(BF16)
                out_ref[1] = v_acc[:, columns].astype(BF16)


def attend_kernel(tiles_ref, bits_ref, q_ref, own_ref, other_ref, out_ref):
    tiles, piece, _ = q_ref.shape
    text = 16
    rows = piece - TAIL
    group = rows // text
    vis = own_ref.shape[1]
    together = TOGETHER
    columns = lax.broadcasted_iota(jnp.int32, (text, vis), 1).astype(F32)

    def step(number, _):
        first = number * together
        lines = []
        for at in range(together):
            digits = q_ref[first + at, rows:, :].astype(F32)
            lines.append(digits[0:1] * 512 + digits[1:2] * 2 + digits[2:3])
            lines.append(digits[3:4] * 512 + digits[4:5] * 2 + digits[5:6])
        edges = jnp.concatenate(lines, axis=0).T[:text]
        queries = jnp.concatenate([q_ref[first + at, :rows, :] for at in range(together)], axis=0)
        scores, tops = [], []
        for source, kv_ref in enumerate((own_ref, other_ref)):
            start = (tiles_ref[source] * vis).astype(F32)
            found = lax.dot_general(
                queries, kv_ref[0], (((1,), (1,)), ((), ())), preferred_element_type=F32
            ).reshape(together, group, text, vis)
            parts = []
            for at in range(together):
                lower, upper = edges[:, 2 * at:2 * at + 1], edges[:, 2 * at + 1:2 * at + 2]
                hidden = (1 - bits_ref[source, first + at]).astype(F32) * 1e7
                visible = (columns >= lower - start + hidden) & (columns < upper - start)
                bias = jnp.where(visible, 0.0, HIDDEN)
                parts.append(found[at] + bias[None])
            masked = jnp.stack(parts).reshape(together * rows, vis)
            scores.append(masked)
            tops.append(jnp.max(masked, axis=1, keepdims=True))
        top = jnp.maximum(jnp.maximum(tops[0], tops[1]), FLOOR)
        total = jnp.zeros((together * rows, 1), F32)
        summed = jnp.zeros((together * rows, HD), F32)
        for masked, kv_ref in zip(scores, (own_ref, other_ref)):
            weights = jnp.exp2((masked - top) * RATE)
            total += jnp.sum(weights, axis=1, keepdims=True)
            summed += jnp.dot(weights.astype(BF16), kv_ref[1], preferred_element_type=F32)
        summed = summed.astype(BF16)
        lanes = lane_ids(LANES)
        for pair in range(together // 2):
            cut = slice(pair * LANES, (pair + 1) * LANES)
            both = jnp.where(lanes == 0, top[cut], jnp.where(lanes == 1, total[cut], 0.0)).T
            both = both[0:8]
            for half in range(2):
                at = 2 * pair + half
                out_ref[first + at, :rows, :] = summed[at * rows:(at + 1) * rows]
                if half:
                    both = pltpu.roll(both, rows, 1)
                out_ref[first + at, rows:, :] = stats_block(both[0:1], both[1:2])
        return 0

    lax.fori_loop(0, tiles // together, step, 0, unroll=UNROLL)


def joined(pieces):
    n = len(pieces)
    rows = pieces[0].shape[0] - TAIL
    stats = [read_stats(piece[rows:, :]) for piece in pieces]
    tops = jnp.concatenate([top for top, _ in stats], axis=0)
    totals = jnp.concatenate([total for _, total in stats], axis=0)
    top = jnp.max(tops, axis=0, keepdims=True)
    factors = jnp.exp2((tops - top) * RATE)
    total = jnp.sum(factors * totals, axis=0, keepdims=True)
    spread = jnp.concatenate([factors, total, jnp.zeros((LANES - n - 1, LANES), F32)], axis=0).T
    summed = jnp.zeros((rows, LANES), F32)
    for s in range(n):
        summed += spread[:rows, s:s + 1] * pieces[s][:rows, :].astype(F32)
    return top, total, spread[:rows, n:n + 1], summed


def join_kernel(in_ref, out_ref):
    top, total, _, summed = joined([in_ref.at[s] for s in range(in_ref.shape[0])])
    piece = jnp.concatenate([summed.astype(BF16), stats_block(top, total)], axis=0)
    for copy in range(out_ref.shape[0]):
        out_ref[copy] = piece


def finish_kernel(in_ref, out_ref):
    sources = in_ref.shape[0]
    text = out_ref.shape[0]
    for side in range(2):
        _, _, total, summed = joined([in_ref.at[s] for s in range(side, sources, 2)])
        result = (summed / total).astype(BF16)
        group = result.shape[0] // text
        for g in range(group):
            first = (side * group + g) * HD
            out_ref[:, first:first + HD] = result[g * text:(g + 1) * text]


def call(kernel, out, in_specs, grant=GRANT):
    return pl.pallas_call(
        kernel, out_shape=jax.ShapeDtypeStruct(out, BF16), in_specs=in_specs, out_specs=VMEM,
        compiler_params=pltpu.CompilerParams(vmem_limit_bytes=grant),
    )


def project(side, visual, key_weight, value_weight):
    vis_rows, depth = visual.shape
    width = key_weight.shape[1]
    chunks, chunk = depth // CHUNK, CHUNK
    anywhere = pl.BlockSpec(memory_space=pl.ANY)
    return pl.pallas_call(
        project_kernel,
        in_specs=[SMEM, anywhere, anywhere, anywhere],
        out_specs=[VMEM, VMEM],
        out_shape=[jax.ShapeDtypeStruct((2, vis_rows, HD), BF16)] * 2,
        scratch_shapes=[
            pltpu.VMEM((chunks, vis_rows, chunk), BF16),
            pltpu.VMEM((chunks, chunk, width), BF16),
            pltpu.VMEM((chunks, chunk, width), BF16),
            pltpu.VMEM((vis_rows, width), F32),
            pltpu.VMEM((vis_rows, width), F32),
            pltpu.SemaphoreType.DMA((chunks, 3)),
        ],
        compiler_params=pltpu.CompilerParams(vmem_limit_bytes=ROOM),
        cost_estimate=pl.CostEstimate(
            flops=4 * vis_rows * depth * width,
            bytes_accessed=2 * depth * (vis_rows + 2 * width),
            transcendentals=0,
        ),
    )(side, visual, key_weight, value_weight)


def per_device(visual, key_weight, value_weight, queries, bounds, tile_mask):
    text = queries.shape[0]
    rows = queries.shape[1] // HD // 2 * text
    piece = rows + TAIL
    zs, ys = lax.axis_size("zh"), lax.axis_size("y")
    phases = lax.axis_size("xh") * 2
    side = lax.axis_index("xl")
    blk = lax.axis_index("zh") * ys + lax.axis_index("y")
    phase = lax.axis_index("xh") * 2 + side
    tiles = jnp.stack([phase * (zs * ys) + blk, (phase ^ 1) * (zs * ys) + blk])
    side = side.reshape(1)

    def exchange(pieces, axis):
        return lax.all_to_all(pieces, axis, 0, 0, tiled=True)

    packed = pl.pallas_call(
        pack_kernel,
        out_shape=jax.ShapeDtypeStruct((zs * ys, piece, LANES), BF16),
        in_specs=[SMEM, VMEM, VMEM],
        out_specs=pl.BlockSpec(memory_space=pl.ANY),
        scratch_shapes=[pltpu.VMEM((piece, LANES), BF16), pltpu.SemaphoreType.DMA((zs * ys,))],
        compiler_params=pltpu.CompilerParams(vmem_limit_bytes=WHOLE),
    )(side, queries, bounds.T)
    gathered = exchange(packed, ("zh", "y"))

    keep, send = project(side, visual, key_weight, value_weight)
    other = lax.ppermute(send, "xl", [(0, 1), (1, 0)])

    tile_ids = lax.broadcasted_iota(jnp.int32, tile_mask.shape, 1)
    bits = jnp.sum(jnp.where(tile_ids[None] == tiles[:, None, None], tile_mask[None], 0), axis=2)
    partials = call(attend_kernel, (zs * ys, piece, LANES), [SMEM, SMEM, VMEM, VMEM, VMEM])(
        tiles, bits, gathered, keep, other
    )
    partials = exchange(partials, ("zh", "y"))
    partials = call(join_kernel, (phases, piece, LANES), [VMEM])(partials)
    partials = exchange(partials, ("xh", "xl"))
    return call(finish_kernel, queries.shape, [VMEM])(partials)


def solution(mesh):
    phases, blocks, heads = (mesh.shape[name] for name in ("phase", "blk", "head"))
    fine = jax.sharding.Mesh(
        mesh.devices.reshape(phases // 2, 2, blocks // 8, 8, heads), ("xh", "xl", "zh", "y", "head")
    )
    phase, blk = ("xh", "xl"), ("zh", "y")
    return jax.shard_map(
        per_device,
        mesh=fine,
        in_specs=(
            P(phase + blk, None),
            P(None, "head"),
            P(None, "head"),
            P(blk, "head"),
            P(blk, None),
            P(),
        ),
        out_specs=P(blk, "head"),
        check_vma=False,
    )
```
